32 devices in a mesh: cache: 2 (over y), tp: 8 (over z, core), cand: 2 (over x).
Axes of the slice: x: 2, y: 2, z: 4, core: 2. Of those that a mesh axis runs over, the one named last changes fastest.
Arguments:
- prompt_inputs: bfloat16 [1536, 8192], P(('cache', 'cand')), may hold values from -6 to 6
- cand_inputs: bfloat16 [4096, 8192], P(('cache', 'cand'), 'tp'), may hold values from -6 to 6
- norm_gain: float32 [8192], replicated, may hold values from 0.1 to 1.9
- w_query: bfloat16 [8192, 8192], P('cache', 'tp'), may hold values from -0.0625 to 0.0625
- w_key: bfloat16 [8192, 1024], P('cache', 'tp'), may hold values from -0.0625 to 0.0625
- w_value: bfloat16 [8192, 1024], P('cache', 'tp'), may hold values from -0.0625 to 0.0625
- q_bias: float32 [8192], P('tp'), may hold values from -180 to 180
- k_bias: float32 [1024], P('tp'), may hold values from -3 to 8
- v_bias: float32 [1024], P('tp'), may hold values from -4 to 4
- cand_lengths: int32 [16], replicated, may hold values from 32 to 256, as said below
- prefix_ends: int32 [16], replicated, may hold values from 384 to 1536, as said below
Outputs:
- attn_out: bfloat16 [4096, 8192], P(('cache', 'cand'), 'tp')
The draws below stay inside these ranges and needn't reach their ends.
Inputs may be any that keep to these rules, and one draw needn't show every extreme that they name: `cand_lengths`: at least one candidate has 256 tokens. `prefix_ends`: at least one candidate follows the whole prompt.
All inputs are finite; a program needn't handle non-finite values.
Results may differ from the reference program's by a relative error of at most 0.0075.
The reference program's roundings to bfloat16 on the way count: a program that leaves them out, or rounds other values in their place, can miss the bound.
Values may be sent and summed in bfloat16 or wider, within the bound.
A program may use at most 192 MiB of HBM per device.

```python
import jax
import jax.numpy as jnp
from jax import lax

D = 8192
HEADS = 64
KV_HEADS = 8
HEAD = 128
CANDS = 16
CLEN = 256
PROMPT = 1536
CTOK = 4096


def draw_q_bias(key, part):
    drawn = jnp.clip(0.5 * jax.random.normal(key, (HEADS * HEAD,), jnp.float32), -3.0, 3.0)
    return drawn


def draw_k_bias(key, part):
    drawn = jnp.clip(0.5 * jax.random.normal(key, (KV_HEADS * HEAD,), jnp.float32), -3.0, 3.0)
    return drawn


def draw_cand_lengths(key, part):
    lengths = jax.random.randint(key, (CANDS,), CLEN // 8, CLEN + 1)
    chosen = jax.random.randint(jax.random.fold_in(key, 3), (), 0, CANDS)
    return jnp.where(jnp.arange(CANDS) == chosen, CLEN, lengths).astype(jnp.int32)


def draw_prefix_ends(key, part):
    prefixes = jax.random.randint(key, (CANDS,), PROMPT // 4, PROMPT + 1)
    chosen = jax.random.randint(jax.random.fold_in(key, 5), (), 0, CANDS)
    return jnp.where(jnp.arange(CANDS) == chosen, PROMPT, prefixes).astype(jnp.int32)


def shard_levels(rng, shape, pieces, smallest, high):
    def one(dim, parts):
        draws = jax.random.uniform(jax.random.fold_in(jax.random.fold_in(rng, 6), dim), (parts,), jnp.float32, smallest / len(pieces), high / len(pieces))
        return jnp.repeat(jnp.exp(draws), shape[dim] // parts).reshape((-1,) + (1,) * (len(shape) - dim - 1))

    loudness = one(*pieces[0])
    for cut in pieces[1:]:
        loudness = loudness * one(*cut)
    return loudness


def gaussian(stream_key, extent, scale, bound, pieces=(), kind=jnp.bfloat16):
    entries = jax.random.normal(stream_key, extent, jnp.float32) * scale
    if len(pieces) > 0:
        entries = shard_levels(stream_key, extent, pieces, -0.22, 0.18) * entries
    return jnp.clip(entries, min=-bound, max=bound).astype(kind)


def setup_inputs(seed: int = 0) -> dict:
    arg_keys = jax.random.split(jax.random.key(seed), 12)
    return {
        "prompt_inputs": gaussian(arg_keys[0], (PROMPT, D), 1.0, 6.0, ((0, 4),)),
        "cand_inputs": gaussian(arg_keys[1], (CTOK, D), 1.0, 6.0, ((0, 4), (1, 8))),
        "norm_gain": jnp.clip(1.0 + 0.18 * jax.random.normal(arg_keys[2], (D,), jnp.float32), 0.1, 1.9),
        "w_query": gaussian(arg_keys[3], (D, HEADS * HEAD), D ** -0.5, 0.0625, ((0, 2), (1, 8))),
        "w_key": gaussian(arg_keys[4], (D, KV_HEADS * HEAD), D ** -0.5, 0.0625, ((0, 2), (1, 8))),
        "w_value": gaussian(arg_keys[5], (D, KV_HEADS * HEAD), D ** -0.5, 0.0625, ((0, 2), (1, 8))),
        "q_bias": draw_q_bias(jax.random.fold_in(arg_keys[11], 71), 0),
        "k_bias": draw_k_bias(jax.random.fold_in(arg_keys[11], 71), 0),
        "v_bias": gaussian(arg_keys[8], (KV_HEADS * HEAD,), 1.0, 4.0, ((0, 8),), jnp.float32),
        "cand_lengths": draw_cand_lengths(jax.random.fold_in(arg_keys[11], 71), 0),
        "prefix_ends": draw_prefix_ends(jax.random.fold_in(arg_keys[11], 71), 0),
    }


ROPE_THETA = 1000000.0
EPSILON = 1e-06

def rotate(tensor, positions):
    half_size = tensor.shape[-1] // 2
    inverse_freq = jnp.power(ROPE_THETA, -jnp.arange(half_size, dtype=jnp.float32) * 2.0 / tensor.shape[-1])
    angles = positions.astype(jnp.float32)[:, None] * inverse_freq[None, :]
    cosine = jnp.cos(angles)[:, None, :]
    sine_part = jnp.sin(angles)[:, None, :]
    first_half = tensor[..., :half_size]
    second = tensor[..., half_size:]
    return jnp.concatenate([first_half * cosine - second * sine_part, second * cosine + first_half * sine_part], axis=-1)

def rms_rows(inputs, gain_vector):
    widened = inputs.astype(jnp.float32)
    inverse = lax.rsqrt(lax.optimization_barrier(jnp.mean(widened * widened, axis=-1, keepdims=True)) + EPSILON)
    return (widened * inverse * gain_vector).astype(jnp.bfloat16)

def reference(prompt_inputs, cand_inputs, norm_gain, w_query, w_key, w_value, q_bias, k_bias, v_bias, cand_lengths, prefix_ends):
    groups = HEADS // KV_HEADS
    normed_p = rms_rows(prompt_inputs, norm_gain)
    normed_c = rms_rows(cand_inputs, norm_gain)
    prompt_pos = jnp.arange(PROMPT, dtype=jnp.int32)
    cand_rows = jnp.arange(CTOK, dtype=jnp.int32)
    cand_pos = (prefix_ends[cand_rows // CLEN] + cand_rows % CLEN).astype(jnp.int32)

    def keys_of(normed, positions):
        key_part = jnp.dot(normed, w_key, preferred_element_type=jnp.float32) + k_bias
        key_part = rotate(key_part.reshape(-1, KV_HEADS, HEAD), positions).astype(jnp.bfloat16)
        value_part = (jnp.dot(normed, w_value, preferred_element_type=jnp.float32) + v_bias).astype(jnp.bfloat16)
        return (lax.optimization_barrier(key_part), lax.optimization_barrier(value_part.reshape(-1, KV_HEADS, HEAD)))
    keys_p, values_p = keys_of(normed_p, prompt_pos)
    keys_c, values_c = keys_of(normed_c, cand_pos)
    queries = jnp.dot(normed_c, w_query, preferred_element_type=jnp.float32) + q_bias
    queries = rotate(queries.reshape(CTOK, HEADS, HEAD), cand_pos).astype(jnp.bfloat16)
    queries = lax.optimization_barrier(queries).reshape(CANDS, CLEN, KV_HEADS, groups, HEAD)
    keys_c = keys_c.reshape(CANDS, CLEN, KV_HEADS, HEAD)
    values_c = values_c.reshape(CANDS, CLEN, KV_HEADS, HEAD)
    scaling = HEAD ** (-0.5)

    def per_item(item_index):
        cand_index = item_index // KV_HEADS
        head_index = item_index % KV_HEADS
        query_rows = queries[cand_index, :, head_index].astype(jnp.float32)
        key_rows = jnp.concatenate([keys_p[:, head_index], keys_c[cand_index, :, head_index]], 0).astype(jnp.float32)
        value_rows = jnp.concatenate([values_p[:, head_index], values_c[cand_index, :, head_index]], 0).astype(jnp.float32)
        scores = jnp.einsum('rqd,nd->rqn', query_rows, key_rows) * scaling
        key_ids = jnp.arange(PROMPT + CLEN, dtype=jnp.int32)
        row_ids = jnp.arange(CLEN, dtype=jnp.int32)
        visible = jnp.where(key_ids[None, :] < PROMPT, key_ids[None, :] < prefix_ends[cand_index], key_ids[None, :] - PROMPT <= row_ids[:, None])
        scores = jnp.where(visible[:, None, :], scores, -jnp.inf)
        maxima = lax.optimization_barrier(jnp.max(scores, axis=-1, keepdims=True))
        weights = jnp.exp(scores - maxima)
        totals = lax.optimization_barrier(jnp.sum(weights, axis=-1))
        rounded = lax.optimization_barrier(weights.astype(jnp.bfloat16)).astype(jnp.float32)
        output = jnp.einsum('rqn,nd->rqd', rounded, value_rows) / totals[..., None]
        output = jnp.where((row_ids < cand_lengths[cand_index])[:, None, None], output, 0.0)
        return output.astype(jnp.bfloat16)
    results = lax.map(per_item, jnp.arange(CANDS * KV_HEADS, dtype=jnp.int32))
    results = results.reshape(CANDS, KV_HEADS, CLEN, groups, HEAD).transpose(0, 2, 1, 3, 4)
    return results.reshape(CTOK, HEADS * HEAD)
```

```python
import functools
import math

import jax
import jax.numpy as jnp
from jax import lax
from jax.experimental import pallas as pl
from jax.experimental.pallas import tpu as pltpu
from jax.sharding import PartitionSpec as P

D = 8192
HEADS = 64
KV_HEADS = 8
HEAD = 128
CANDS = 16
CLEN = 256


ROPE_THETA = 1000000.0
EPSILON = 1e-06


def rotate(tensor, positions):
    half_size = tensor.shape[-1] // 2
    inverse_freq = jnp.power(
        ROPE_THETA, -jnp.arange(half_size, dtype=jnp.float32) * 2.0 / tensor.shape[-1]
    )
    angles = positions.astype(jnp.float32)[:, None] * inverse_freq[None, :]
    cosine = jnp.cos(angles)[:, None, :]
    sine_part = jnp.sin(angles)[:, None, :]
    first_half = tensor[..., :half_size]
    second = tensor[..., half_size:]
    return jnp.concatenate(
        [first_half * cosine - second * sine_part, second * cosine + first_half * sine_part],
        axis=-1,
    )


def row_lookup(row_ids, table):
    chosen = (row_ids // CLEN)[:, None] == jnp.arange(CANDS, dtype=jnp.int32)[None, :]
    return jnp.sum(jnp.where(chosen, table[None, :], 0), axis=1)


def attend_kernel(
    prefix_ref, length_ref, offset_ref, q_ref, kvp_ref, kvc_ref, out_ref, *, heads, chunk, scale
):
    cand = pl.program_id(0)
    prefix = prefix_ref[cand]
    length = length_ref[cand]
    offset = offset_ref[cand]
    rows = q_ref.shape[0]
    contract = (((1,), (1,)), ((), ()))

    def scores_of(head, key_rows):
        return (
            lax.dot_general(
                q_ref[:, head * HEAD : (head + 1) * HEAD],
                key_rows,
                contract,
                preferred_element_type=jnp.float32,
            )
            * scale
        )

    def weighted(probabilities, value_rows):
        return jnp.dot(
            probabilities.astype(jnp.bfloat16), value_rows, preferred_element_type=jnp.float32
        )

    own_shape = (rows, kvc_ref.shape[0])
    causal = lax.broadcasted_iota(jnp.int32, own_shape, 1) <= offset + lax.broadcasted_iota(
        jnp.int32, own_shape, 0
    )
    state = []
    for head in range(heads):
        scores = jnp.where(causal, scores_of(head, kvc_ref[:, :HEAD]), -1e30)
        maxima = jnp.max(scores, axis=1, keepdims=True)
        probabilities = jnp.exp2(scores - maxima)
        totals = jnp.sum(probabilities, axis=1, keepdims=True)
        state += [maxima, totals, weighted(probabilities, kvc_ref[:, HEAD:])]

    def advance(turn, running):
        first = pl.multiple_of(turn * chunk, chunk)
        key_rows = kvp_ref[pl.ds(first, chunk), :HEAD]
        value_rows = kvp_ref[pl.ds(first, chunk), HEAD:]
        seen = first + lax.broadcasted_iota(jnp.int32, (rows, chunk), 1) < prefix
        following = []
        for head in range(heads):
            maxima, totals, accumulated = running[3 * head : 3 * head + 3]
            scores = jnp.where(seen, scores_of(head, key_rows), -1e30)
            new_maxima = jnp.maximum(maxima, jnp.max(scores, axis=1, keepdims=True))
            probabilities = jnp.exp2(scores - new_maxima)
            rescale = jnp.exp2(maxima - new_maxima)
            totals = totals * rescale + jnp.sum(probabilities, axis=1, keepdims=True)
            accumulated = accumulated * rescale + weighted(probabilities, value_rows)
            following += [new_maxima, totals, accumulated]
        return tuple(following)

    state = lax.fori_loop(0, (prefix + chunk - 1) // chunk, advance, tuple(state))
    valid = offset + lax.broadcasted_iota(jnp.int32, (rows, HEAD), 0) < length
    for head in range(heads):
        result = state[3 * head + 2] / state[3 * head + 1]
        out_ref[:, head * HEAD : (head + 1) * HEAD] = jnp.where(valid, result, 0.0).astype(
            jnp.bfloat16
        )


def attend(prefixes, lengths, offsets, queries, kv_prompt, kv_cand, kv_local, groups):
    tiles = prefixes.shape[0]
    rows = queries.shape[0] // tiles
    prompt = kv_prompt.shape[0]
    chunk = next(size for size in (512, 256, 128, prompt) if prompt % size == 0)
    heads = 2 if groups % 2 == 0 else 1
    turns = groups // heads
    return pl.pallas_call(
        functools.partial(
            attend_kernel, heads=heads, chunk=chunk, scale=HEAD ** (-0.5) * math.log2(math.e)
        ),
        grid_spec=pltpu.PrefetchScalarGridSpec(
            num_scalar_prefetch=3,
            grid=(tiles, kv_local, turns),
            in_specs=[
                pl.BlockSpec((rows, heads * HEAD), lambda c, k, t, *_: (c, k * turns + t)),
                pl.BlockSpec((prompt, 2 * HEAD), lambda c, k, t, *_: (0, k)),
                pl.BlockSpec((CLEN, 2 * HEAD), lambda c, k, t, *_: (c, k)),
            ],
            out_specs=pl.BlockSpec((rows, heads * HEAD), lambda c, k, t, *_: (c, k * turns + t)),
        ),
        out_shape=jax.ShapeDtypeStruct(queries.shape, jnp.bfloat16),
        cost_estimate=pl.CostEstimate(
            flops=4 * queries.size * (prompt + CLEN),
            bytes_accessed=4 * queries.size,
            transcendentals=queries.size // HEAD * (prompt + CLEN),
        ),
        compiler_params=pltpu.CompilerParams(vmem_limit_bytes=60 * 1024 * 1024),
    )(prefixes, lengths, offsets, queries, kv_prompt, kv_cand)


def query_product(normed, w_query):
    caches = lax.axis_size("cache")
    cands = lax.axis_size("cand")
    depth = w_query.shape[0]
    if caches != 2 or cands != 2 or depth % 4 != 0:
        return jnp.dot(
            normed,
            lax.all_gather(w_query, "cache", axis=0, tiled=True),
            preferred_element_type=jnp.float32,
        )
    mine = lax.axis_index("cache")
    side = lax.axis_index("cand")
    part = depth // 4
    swap = [(0, 1), (1, 0)]
    direct = [
        lax.ppermute(
            lax.dynamic_slice_in_dim(w_query, (2 * side + turn) * part, part), "cache", swap
        )
        for turn in range(2)
    ]
    relayed = [lax.ppermute(piece, "cand", swap) for piece in direct]

    def product(first, weights):
        columns = lax.dynamic_slice_in_dim(normed, first, weights.shape[0], 1)
        return jnp.dot(columns, weights, preferred_element_type=jnp.float32)

    total = product(mine * depth, w_query)
    other = (1 - mine) * depth
    for turn in range(2):
        total = total + product(other + (2 * side + turn) * part, direct[turn])
    for turn in range(2):
        total = total + product(other + (2 * (1 - side) + turn) * part, relayed[turn])
    return total


def per_device(
    prompt_inputs,
    cand_inputs,
    norm_gain,
    w_query,
    w_key,
    w_value,
    q_bias,
    k_bias,
    v_bias,
    cand_lengths,
    prefix_ends,
):
    prompt_dev = prompt_inputs.shape[0]
    cand_dev = cand_inputs.shape[0]
    head_size = HEAD
    kv_local = w_key.shape[1] // head_size
    groups = HEADS // KV_HEADS
    kv_width = kv_local * head_size
    joined = lax.axis_index("cache") * lax.axis_size("cand") + lax.axis_index("cand")
    widened_p = prompt_inputs.astype(jnp.float32)
    normed_p = (
        widened_p
        * lax.rsqrt(jnp.mean(widened_p * widened_p, axis=-1, keepdims=True) + EPSILON)
        * norm_gain
    ).astype(jnp.bfloat16)
    widened_c = cand_inputs.astype(jnp.float32)
    squares = lax.psum(jnp.sum(widened_c * widened_c, axis=-1), "tp")
    part_width = cand_inputs.shape[1]
    gain_part = lax.dynamic_slice_in_dim(norm_gain, lax.axis_index("tp") * part_width, part_width)
    normed_part = (widened_c * lax.rsqrt(squares / D + EPSILON)[:, None] * gain_part).astype(
        jnp.bfloat16
    )
    normed_c = lax.all_gather(normed_part, "tp", axis=1, tiled=True)
    row_ids = joined * cand_dev + jnp.arange(cand_dev, dtype=jnp.int32)
    prefix_row = row_lookup(row_ids, prefix_ends)
    cand_pos = prefix_row + row_ids % CLEN
    prompt_pos = joined * prompt_dev + jnp.arange(prompt_dev, dtype=jnp.int32)
    key_value = jnp.concatenate([w_key, w_value], axis=1)
    key_value = lax.all_gather(key_value, "cache", axis=0, tiled=True)
    kv_prompt = jnp.dot(normed_p, key_value, preferred_element_type=jnp.float32)

    def keys_values(product, positions):
        rows = product.shape[0]
        keys = rotate(
            (product[:, :kv_width] + k_bias).reshape(rows, kv_local, head_size), positions
        ).astype(jnp.bfloat16)
        values = (product[:, kv_width:] + v_bias).astype(jnp.bfloat16)
        values = values.reshape(rows, kv_local, head_size)
        return jnp.concatenate([keys, values], axis=2).reshape(rows, 2 * kv_width)

    kv_p = lax.all_gather(
        keys_values(kv_prompt, prompt_pos), ("cache", "cand"), axis=0, tiled=True
    )
    q_cand = query_product(normed_c, w_query)
    kv_c = keys_values(jnp.dot(normed_c, key_value, preferred_element_type=jnp.float32), cand_pos)
    queries = rotate(
        (q_cand + q_bias).reshape(cand_dev, kv_local * groups, head_size), cand_pos
    ).astype(jnp.bfloat16)
    tile_rows = min(cand_dev, CLEN)
    tile_first = joined * cand_dev + tile_rows * jnp.arange(cand_dev // tile_rows, dtype=jnp.int32)
    prefixes = row_lookup(tile_first, prefix_ends)
    lengths = row_lookup(tile_first, cand_lengths)
    offsets = tile_first % CLEN
    if cand_dev < CLEN:
        kv_c = lax.all_gather(kv_c, ("cache", "cand"), axis=0, tiled=True)
        kv_c = lax.dynamic_slice_in_dim(kv_c, joined * cand_dev // CLEN * CLEN, CLEN)
    return attend(
        prefixes,
        lengths,
        offsets,
        queries.reshape(cand_dev, kv_local * groups * head_size),
        kv_p,
        kv_c,
        kv_local,
        groups,
    )


def solution(mesh):
    placed = (
        P(("cache", "cand"), None),
        P(("cache", "cand"), "tp"),
        P(),
        P("cache", "tp"),
        P("cache", "tp"),
        P("cache", "tp"),
        P("tp"),
        P("tp"),
        P("tp"),
        P(),
        P(),
    )
    return jax.shard_map(
        per_device,
        mesh=mesh,
        in_specs=placed,
        out_specs=P(("cache", "cand"), "tp"),
        check_vma=False,
    )
```

```python
import functools
import math

import jax
import jax.numpy as jnp
from jax import lax
from jax.experimental import pallas as pl
from jax.experimental.pallas import tpu as pltpu
from jax.sharding import PartitionSpec as P

D = 8192
HEADS = 64
KV_HEADS = 8
HEAD = 128
CANDS = 16
CLEN = 256


ROPE_THETA = 1000000.0
EPSILON = 1e-06


def rotate(tensor, positions):
    half_size = tensor.shape[-1] // 2
    inverse_freq = jnp.power(
        ROPE_THETA, -jnp.arange(half_size, dtype=jnp.float32) * 2.0 / tensor.shape[-1]
    )
    angles = positions.astype(jnp.float32)[:, None] * inverse_freq[None, :]
    cosine = jnp.cos(angles)[:, None, :]
    sine_part = jnp.sin(angles)[:, None, :]
    first_half = tensor[..., :half_size]
    second = tensor[..., half_size:]
    return jnp.concatenate(
        [first_half * cosine - second * sine_part, second * cosine + first_half * sine_part],
        axis=-1,
    )


def row_lookup(row_ids, table):
    chosen = (row_ids // CLEN)[:, None] == jnp.arange(CANDS, dtype=jnp.int32)[None, :]
    return jnp.sum(jnp.where(chosen, table[None, :], 0), axis=1)


def attend_kernel(
    prefix_ref, length_ref, offset_ref, q_ref, kvp_ref, kvc_ref, out_ref, *, heads, chunk, scale
):
    cand = pl.program_id(0)
    prefix = prefix_ref[cand]
    length = length_ref[cand]
    offset = offset_ref[cand]
    rows = q_ref.shape[0]
    contract = (((1,), (1,)), ((), ()))

    def scores_of(head, key_rows):
        return (
            lax.dot_general(
                q_ref[:, head * HEAD : (head + 1) * HEAD],
                key_rows,
                contract,
                preferred_element_type=jnp.float32,
            )
            * scale
        )

    def weighted(probabilities, value_rows):
        return jnp.dot(
            probabilities.astype(jnp.bfloat16), value_rows, preferred_element_type=jnp.float32
        )

    own_shape = (rows, kvc_ref.shape[0])
    causal = lax.broadcasted_iota(jnp.int32, own_shape, 1) <= offset + lax.broadcasted_iota(
        jnp.int32, own_shape, 0
    )
    state = []
    for head in range(heads):
        scores = jnp.where(causal, scores_of(head, kvc_ref[:, :HEAD]), -1e30)
        maxima = jnp.max(scores, axis=1, keepdims=True)
        probabilities = jnp.exp2(scores - maxima)
        totals = jnp.sum(probabilities, axis=1, keepdims=True)
        state += [maxima, totals, weighted(probabilities, kvc_ref[:, HEAD:])]

    def advance(turn, running):
        first = pl.multiple_of(turn * chunk, chunk)
        key_rows = kvp_ref[pl.ds(first, chunk), :HEAD]
        value_rows = kvp_ref[pl.ds(first, chunk), HEAD:]
        seen = first + lax.broadcasted_iota(jnp.int32, (rows, chunk), 1) < prefix
        following = []
        for head in range(heads):
            maxima, totals, accumulated = running[3 * head : 3 * head + 3]
            scores = jnp.where(seen, scores_of(head, key_rows), -1e30)
            new_maxima = jnp.maximum(maxima, jnp.max(scores, axis=1, keepdims=True))
            probabilities = jnp.exp2(scores - new_maxima)
            rescale = jnp.exp2(maxima - new_maxima)
            totals = totals * rescale + jnp.sum(probabilities, axis=1, keepdims=True)
            accumulated = accumulated * rescale + weighted(probabilities, value_rows)
            following += [new_maxima, totals, accumulated]
        return tuple(following)

    state = lax.fori_loop(0, (prefix + chunk - 1) // chunk, advance, tuple(state))
    valid = offset + lax.broadcasted_iota(jnp.int32, (rows, HEAD), 0) < length
    for head in range(heads):
        result = state[3 * head + 2] / state[3 * head + 1]
        out_ref[:, head * HEAD : (head + 1) * HEAD] = jnp.where(valid, result, 0.0).astype(
            jnp.bfloat16
        )


def attend(prefixes, lengths, offsets, queries, kv_prompt, kv_cand, kv_local, groups):
    tiles = prefixes.shape[0]
    rows = queries.shape[0] // tiles
    prompt = kv_prompt.shape[0]
    chunk = next(size for size in (512, 256, 128, prompt) if prompt % size == 0)
    heads = 2 if groups % 2 == 0 else 1
    turns = groups // heads
    return pl.pallas_call(
        functools.partial(
            attend_kernel, heads=heads, chunk=chunk, scale=HEAD ** (-0.5) * math.log2(math.e)
        ),
        grid_spec=pltpu.PrefetchScalarGridSpec(
            num_scalar_prefetch=3,
            grid=(tiles, kv_local, turns),
            in_specs=[
                pl.BlockSpec((rows, heads * HEAD), lambda c, k, t, *_: (c, k * turns + t)),
                pl.BlockSpec((prompt, 2 * HEAD), lambda c, k, t, *_: (0, k)),
                pl.BlockSpec((CLEN, 2 * HEAD), lambda c, k, t, *_: (c, k)),
            ],
            out_specs=pl.BlockSpec((rows, heads * HEAD), lambda c, k, t, *_: (c, k * turns + t)),
        ),
        out_shape=jax.ShapeDtypeStruct(queries.shape, jnp.bfloat16),
        cost_estimate=pl.CostEstimate(
            flops=4 * queries.size * (prompt + CLEN),
            bytes_accessed=4 * queries.size,
            transcendentals=queries.size // HEAD * (prompt + CLEN),
        ),
        compiler_params=pltpu.CompilerParams(vmem_limit_bytes=60 * 1024 * 1024),
    )(prefixes, lengths, offsets, queries, kv_prompt, kv_cand)


def query_product(normed, w_query):
    caches = lax.axis_size("cache")
    cands = lax.axis_size("cand")
    depth = w_query.shape[0]
    if caches != 2 or cands != 2 or depth % 4 != 0:
        return jnp.dot(
            normed,
            lax.all_gather(w_query, "cache", axis=0, tiled=True),
            preferred_element_type=jnp.float32,
        )
    mine = lax.axis_index("cache")
    side = lax.axis_index("cand")
    part = depth // 4
    swap = [(0, 1), (1, 0)]
    direct = [
        lax.ppermute(
            lax.dynamic_slice_in_dim(w_query, (2 * side + turn) * part, part), "cache", swap
        )
        for turn in range(2)
    ]
    relayed = [lax.ppermute(piece, "cand", swap) for piece in direct]

    def product(first, weights):
        columns = lax.dynamic_slice_in_dim(normed, first, weights.shape[0], 1)
        return jnp.dot(columns, weights, preferred_element_type=jnp.float32)

    total = product(mine * depth, w_query)
    other = (1 - mine) * depth
    for turn in range(2):
        total = total + product(other + (2 * side + turn) * part, direct[turn])
    for turn in range(2):
        total = total + product(other + (2 * (1 - side) + turn) * part, relayed[turn])
    return total


def per_device(
    prompt_inputs,
    cand_inputs,
    norm_gain,
    w_query,
    w_key,
    w_value,
    q_bias,
    k_bias,
    v_bias,
    cand_lengths,
    prefix_ends,
):
    prompt_dev = prompt_inputs.shape[0]
    cand_dev = cand_inputs.shape[0]
    head_size = HEAD
    kv_local = w_key.shape[1] // head_size
    groups = HEADS // KV_HEADS
    kv_width = kv_local * head_size
    joined = lax.axis_index("cache") * lax.axis_size("cand") + lax.axis_index("cand")
    widened_p = prompt_inputs.astype(jnp.float32)
    normed_p = (
        widened_p
        * lax.rsqrt(jnp.mean(widened_p * widened_p, axis=-1, keepdims=True) + EPSILON)
        * norm_gain
    ).astype(jnp.bfloat16)
    widened_c = cand_inputs.astype(jnp.float32)
    squares = lax.psum(jnp.sum(widened_c * widened_c, axis=-1), "tp")
    part_width = cand_inputs.shape[1]
    gain_part = lax.dynamic_slice_in_dim(norm_gain, lax.axis_index("tp") * part_width, part_width)
    normed_part = (widened_c * lax.rsqrt(squares / D + EPSILON)[:, None] * gain_part).astype(
        jnp.bfloat16
    )
    normed_c = lax.all_gather(normed_part, "tp", axis=1, tiled=True)
    row_ids = joined * cand_dev + jnp.arange(cand_dev, dtype=jnp.int32)
    prefix_row = row_lookup(row_ids, prefix_ends)
    cand_pos = prefix_row + row_ids % CLEN
    prompt_pos = joined * prompt_dev + jnp.arange(prompt_dev, dtype=jnp.int32)
    key_value = jnp.concatenate([w_key, w_value], axis=1)
    if lax.axis_size("cache") == 2:
        other_half = lax.ppermute(key_value, "cache", [(0, 1), (1, 0)])
        key_value = jnp.where(
            lax.axis_index("cache") == 0,
            jnp.concatenate([key_value, other_half], axis=0),
            jnp.concatenate([other_half, key_value], axis=0),
        )
    else:
        key_value = lax.all_gather(key_value, "cache", axis=0, tiled=True)
    kv_prompt = jnp.dot(normed_p, key_value, preferred_element_type=jnp.float32)

    def keys_values(product, positions):
        rows = product.shape[0]
        keys = rotate(
            (product[:, :kv_width] + k_bias).reshape(rows, kv_local, head_size), positions
        ).astype(jnp.bfloat16)
        values = (product[:, kv_width:] + v_bias).astype(jnp.bfloat16)
        values = values.reshape(rows, kv_local, head_size)
        return jnp.concatenate([keys, values], axis=2).reshape(rows, 2 * kv_width)

    kv_p = lax.all_gather(
        keys_values(kv_prompt, prompt_pos), ("cache", "cand"), axis=0, tiled=True
    )
    q_cand = query_product(normed_c, w_query)
    kv_c = keys_values(jnp.dot(normed_c, key_value, preferred_element_type=jnp.float32), cand_pos)
    queries = rotate(
        (q_cand + q_bias).reshape(cand_dev, kv_local * groups, head_size), cand_pos
    ).astype(jnp.bfloat16)
    tile_rows = min(cand_dev, CLEN)
    tile_first = joined * cand_dev + tile_rows * jnp.arange(cand_dev // tile_rows, dtype=jnp.int32)
    prefixes = row_lookup(tile_first, prefix_ends)
    lengths = row_lookup(tile_first, cand_lengths)
    offsets = tile_first % CLEN
    if cand_dev < CLEN:
        kv_c = lax.all_gather(kv_c, ("cache", "cand"), axis=0, tiled=True)
        kv_c = lax.dynamic_slice_in_dim(kv_c, joined * cand_dev // CLEN * CLEN, CLEN)
    return attend(
        prefixes,
        lengths,
        offsets,
        queries.reshape(cand_dev, kv_local * groups * head_size),
        kv_p,
        kv_c,
        kv_local,
        groups,
    )


def solution(mesh):
    placed = (
        P(("cache", "cand"), None),
        P(("cache", "cand"), "tp"),
        P(),
        P("cache", "tp"),
        P("cache", "tp"),
        P("cache", "tp"),
        P("tp"),
        P("tp"),
        P("tp"),
        P(),
        P(),
    )
    return jax.shard_map(
        per_device,
        mesh=mesh,
        in_specs=placed,
        out_specs=P(("cache", "cand"), "tp"),
        check_vma=False,
    )
```
